512 devices in a mesh: dp: 8 (over y, x_lo), expert: 64 (over z, x_hi, core).
Axes of the slice: x: 4 (x_hi: 2, x_lo: 2; x = x_hi * 2 + x_lo), y: 4, z: 16, core: 2. Of those that a mesh axis runs over, the one named last changes fastest.
Arguments:
- tokens: bfloat16 [65536, 2048], P(('dp', 'expert')), may hold values from -6 to 6
- routes: int32 [65536, 2], P(('dp', 'expert')), may hold values from 0 to 63, all different within a row; in each aligned block of 128 rows (0 to 127, 128 to 255, ...) at most 6 rows name the same one
- gates: float32 [65536, 2], P(('dp', 'expert')), may hold values from 0.05 to 1
- grad_out: bfloat16 [65536, 2048], P(('dp', 'expert')), may hold values from -6 to 6
- w_gate: bfloat16 [64, 2048, 768], P('expert', 'dp'), may hold values from -0.125 to 0.125
- w_up: bfloat16 [64, 2048, 768], P('expert', 'dp'), may hold values from -0.125 to 0.125
- w_down: bfloat16 [64, 768, 2048], P('expert', None, 'dp'), may hold values from -0.21875 to 0.21875
Outputs:
- grad_tokens: bfloat16 [65536, 2048], P(('dp', 'expert'))
- grad_gates: float32 [65536, 2], P(('dp', 'expert'))
- grad_down: float32 [64, 768, 2048], P('expert', None, 'dp')
The draws below stay inside these ranges and needn't reach their ends.
Inputs may be any that keep to these rules, and one draw needn't show every extreme that they name: Within the rows of one device no expert is named by more than 6 routes, a bound that some block reaches; the 2 experts of a token differ.
All inputs are finite; a program needn't handle non-finite values.
Results may differ from the reference program's by a relative error of at most 0.015.
Values may be sent and summed in bfloat16 or wider, within the bound.
A program may use at most 128 MiB of HBM per device.

```python
import math
import jax
import jax.numpy as jnp
import numpy as np
from jax import lax

D = 2048
H = 768
TOP = 2
TOK_DEV = 128
EXPERTS = 64
CAP = 6
TOKENS = 65536
N_DP = 8
N_EXPERT = 64


def steps_of(rng, extent, split, smallest, largest):
    gain = 1.0
    for dim, shards_of in split:
        draws = jax.random.uniform(jax.random.fold_in(jax.random.fold_in(rng, 6), dim), (shards_of,), jnp.float32, smallest / len(split), largest / len(split))
        gain = gain * jnp.repeat(jnp.exp(draws), extent[dim] // shards_of).reshape((-1,) + (1,) * (len(extent) - 1 - dim))
    return gain


def shared_out(own_key, own, number, rows, count, top, reach, skew):
    sequence = jax.random.permutation(own_key, count)
    heavy_load, usual = load_shares(count, rows * top, reach, skew, True), load_shares(count, rows * top, reach, skew, False)
    places = jnp.arange(count)

    def named(tallies, offset_by):
        used = int((tallies > 0).sum())
        fixed = max(1, used // 4)
        moved = fixed + (places - fixed + offset_by * (used - fixed)) % max(1, count - fixed)
        return jnp.zeros((count,), jnp.int32).at[sequence[jnp.where(places < fixed, places, moved)]].set(jnp.asarray(tallies, jnp.int32))

    tallies = jnp.where(number % 4 == 0, named(heavy_load, number // 4), named(usual, number - number // 4 - 1))
    mixed = jax.random.permutation(jax.random.fold_in(own, 3), count)
    donor, taker = mixed[0:count // 2 * 2:2], mixed[1:count // 2 * 2:2]
    room = jnp.minimum(tallies[donor] - 1, reach - tallies[taker]) // 2
    room = jnp.where((donor == sequence[0]) | (taker == sequence[0]) | (tallies[taker] == 0), 0, jnp.maximum(room, 0))
    moved = jax.random.randint(jax.random.fold_in(own, 4), (count // 2,), 0, 1 << 20) % (room + 1)
    tallies = tallies.at[donor].add(-moved).at[taker].add(moved)
    members = jnp.searchsorted(jnp.cumsum(tallies), jnp.arange(rows * top), side="right").astype(jnp.int32)
    listing = members.reshape(top, rows).T
    listing = listing[jax.random.permutation(jax.random.fold_in(own, 1), rows)]
    offset_by = jax.random.randint(jax.random.fold_in(own, 2), (rows, 1), 0, top)
    return jnp.take_along_axis(listing, (jnp.arange(top)[None, :] + offset_by) % top, axis=1)


def load_shares(count, total, bound, skew, full):
    weights = [(1 << 20) // math.isqrt(rank ** skew) + 1 for rank in range(1, count + 1)]
    largest = bound if full else min(bound, max(-(-total // count), total * weights[0] // sum(weights)))
    least = 1 if total - largest >= count - 1 else 0
    counts, spare = [largest] + [least] * (count - 1), total - largest - least * (count - 1)
    while spare > 0:
        candidates = [i for i in range(1, count) if counts[i] < largest] or [i for i in range(1, count) if counts[i] < bound]
        pool, left = sum([weights[i] for i in candidates]), spare
        for i in candidates:
            more = min(bound - counts[i], max(1, left * weights[i] // pool), spare)
            counts[i] = counts[i] + more
            spare = spare - more
    return np.array(counts)


def bell_draw(rng, extent, width, most, shards=(), held_as=jnp.bfloat16):
    array = jax.random.normal(rng, extent, jnp.float32) * width
    if len(shards) > 0:
        array = steps_of(rng, extent, shards, -0.22, 0.18) * array
    return jnp.clip(array, min=-most, max=most).astype(held_as)


def setup_inputs(seed: int = 0) -> dict:
    seeds = jax.random.split(jax.random.key(seed), 8)
    tokens = bell_draw(seeds[0], (TOKENS, D), 1.0, 6.0, ((0, 512),))
    routes_keys = jax.random.split(jax.random.fold_in(seeds[1], 1), TOKENS // TOK_DEV)
    routes_turns = jax.random.permutation(jax.random.fold_in(seeds[1], 3), TOKENS // TOK_DEV)
    routes = jax.vmap(lambda own, number: shared_out(jax.random.fold_in(seeds[1], 2), own, number, TOK_DEV, EXPERTS, TOP, CAP, 2))(routes_keys, routes_turns).reshape((TOKENS, TOP))
    gates = jnp.clip(jnp.exp(math.log(1.0) - 2.9957323 * jax.random.uniform(seeds[2], (TOKENS, TOP), jnp.float32) ** steps_of(seeds[2], (TOKENS, TOP), ((0, 512),), -0.2, 0.2)), 0.05, 1.0)
    grad_out = bell_draw(seeds[3], (TOKENS, D), 1.0, 6.0, ((0, 512),))
    w_gate = bell_draw(seeds[4], (EXPERTS, D, H), D ** -0.5, 0.125, ((0, 64), (1, 8)))
    w_up = bell_draw(seeds[5], (EXPERTS, D, H), D ** -0.5, 0.125, ((0, 64), (1, 8)))
    w_down = bell_draw(seeds[6], (EXPERTS, H, D), H ** -0.5, 0.21875, ((0, 64), (2, 8)))
    return {"tokens": tokens, "routes": routes, "gates": gates, "grad_out": grad_out, "w_gate": w_gate, "w_up": w_up, "w_down": w_down}


def silu_parts(pre):
    sig = jax.nn.sigmoid(pre)
    return pre * sig, sig * (1.0 + pre * (1.0 - sig))


def contract_last(left, right):
    return lax.dot_general(left, right, (((1,), (1,)), ((), ())), preferred_element_type=jnp.float32)


def reference(tokens, routes, gates, grad_out, w_gate, w_up, w_down):
    devices = N_DP * N_EXPERT
    flat = routes.reshape(-1).astype(jnp.int32)
    routed = TOKENS * TOP
    per_dev = TOK_DEV * TOP
    labels = jnp.arange(EXPERTS, dtype=jnp.int32)
    onehot = (flat[:, None] == labels[None, :]).astype(jnp.int32)
    blocked = onehot.reshape(devices, per_dev, EXPERTS)
    rank = (jnp.cumsum(blocked, axis=1) - blocked).reshape(routed, EXPERTS)
    rank = jnp.sum(rank * onehot, axis=1).astype(jnp.int32)
    device = (jnp.arange(routed, dtype=jnp.int32) // per_dev).astype(jnp.int32)
    position = device * CAP + rank
    table = jnp.full((EXPERTS, devices * CAP), routed, jnp.int32)
    table = table.at[flat, position].set(jnp.arange(routed, dtype=jnp.int32))
    padded_tokens = jnp.concatenate([tokens, jnp.zeros((1, D), jnp.bfloat16)], axis=0)
    padded_grads = jnp.concatenate([grad_out, jnp.zeros((1, D), jnp.bfloat16)], axis=0)
    padded_gates = jnp.concatenate([gates.reshape(-1), jnp.ones((1,), jnp.float32)], axis=0)

    def expert_step(carry, inputs):
        total, gate_grad = carry
        index, wg, wu, wd = inputs
        source = (index // TOP).astype(jnp.int32)
        x_rows = padded_tokens[source]
        scale = padded_gates[index]
        scaled = (scale[:, None] * padded_grads[source].astype(jnp.float32)).astype(jnp.bfloat16)
        pre_gate = jnp.dot(x_rows, wg, preferred_element_type=jnp.float32)
        pre_up = jnp.dot(x_rows, wu, preferred_element_type=jnp.float32)
        act, slope = silu_parts(pre_gate)
        hidden_f = act * pre_up
        hidden = hidden_f.astype(jnp.bfloat16)
        back = contract_last(scaled, wd)
        score = lax.optimization_barrier(jnp.sum(back * hidden_f, axis=1).astype(jnp.bfloat16)).astype(jnp.float32)
        d_gate = (back * pre_up * slope).astype(jnp.bfloat16)
        d_up = (back * act).astype(jnp.bfloat16)
        route_grad = (contract_last(d_gate, wg) + contract_last(d_up, wu)).astype(jnp.bfloat16)
        total = total.at[source].add(route_grad.astype(jnp.float32))
        gate_grad = gate_grad.at[index].set(score / scale)
        grouped_h = hidden.reshape(N_DP, N_EXPERT * CAP, H).astype(jnp.float32)
        grouped_s = scaled.reshape(N_DP, N_EXPERT * CAP, D).astype(jnp.float32)
        partial_value = jnp.einsum("gsh,gsd->ghd", grouped_h, grouped_s)
        summed = jnp.sum(lax.optimization_barrier(partial_value.astype(jnp.bfloat16)).astype(jnp.float32), axis=0)
        return (total, gate_grad), summed

    start = (jnp.zeros((TOKENS + 1, D), jnp.float32), jnp.zeros((routed + 1,), jnp.float32))
    (total, gate_grad), grad_down = lax.scan(expert_step, start, (table, w_gate, w_up, w_down))
    grad_tokens = total[:TOKENS].astype(jnp.bfloat16)
    grad_gates = gate_grad[:routed].reshape(TOKENS, TOP)
    return grad_tokens, grad_gates, grad_down
```

```python
import functools

import jax
import jax.numpy as jnp
from jax import lax
from jax.experimental import pallas as pl
from jax.experimental.pallas import tpu as pltpu
from jax.sharding import PartitionSpec as P


def silu_parts(pre):
    sig = jax.nn.sigmoid(pre)
    return (pre * sig, sig * (1.0 + pre * (1.0 - sig)))


def contract_last(left, right):
    return lax.dot_general(
        left, right, (((1,), (1,)), ((), ())), preferred_element_type=jnp.float32
    )


def xfer_kernel(plan, sizes, *refs):
    count = len(plan)
    srcs, dsts = refs[:count], refs[count:2 * count]
    send, recv, own = refs[2 * count:2 * count + 3]
    me_dp = lax.axis_index("dp")
    me_ex = lax.axis_index("expert")
    mine = {"dp": me_dp, "expert": me_ex}

    def block(i, peer):
        return srcs[i].at[peer] if plan[i][0] == "a2a" else srcs[i]

    def remote(i, peer, slot):
        axis = plan[i][1]
        device = (peer, me_ex) if axis == "dp" else (me_dp, peer)
        return pltpu.make_async_remote_copy(
            src_ref=block(i, peer),
            dst_ref=dsts[i].at[slot],
            send_sem=send.at[i, peer],
            recv_sem=recv.at[i, slot],
            device_id=device,
            device_id_type=pl.DeviceIdType.MESH,
        )

    local = []
    for i, (kind, axis) in enumerate(plan):
        me = mine[axis]
        copy = pltpu.make_async_copy(block(i, me), dsts[i].at[me], own.at[i])
        copy.start()
        local.append(copy)
    for i, (kind, axis) in enumerate(plan):
        me, n = mine[axis], sizes[axis]

        @pl.loop(1, n)
        def _(j):
            peer = lax.rem(me + j, n)
            remote(i, peer, me).start()

    for i, (kind, axis) in enumerate(plan):
        me, n = mine[axis], sizes[axis]

        @pl.loop(1, n)
        def _(j):
            peer = lax.rem(me + j, n)
            remote(i, peer, me).wait_send()
            remote(i, peer, peer).wait_recv()

    for copy in local:
        copy.wait()


def exchange(plan, sizes, srcs, dst_shapes):
    count = len(plan)
    most = max(sizes.values())
    return pl.pallas_call(
        functools.partial(xfer_kernel, plan, sizes),
        out_shape=[jax.ShapeDtypeStruct(s, a.dtype) for s, a in zip(dst_shapes, srcs)],
        in_specs=[pl.BlockSpec(memory_space=pl.ANY)] * count,
        out_specs=[pl.BlockSpec(memory_space=pl.ANY)] * count,
        scratch_shapes=[
            pltpu.SemaphoreType.DMA((count, most)),
            pltpu.SemaphoreType.DMA((count, most)),
            pltpu.SemaphoreType.DMA((count,)),
        ],
        compiler_params=pltpu.CompilerParams(has_side_effects=True),
    )(*srcs)


def per_device(tokens, routes, gates, grad_out, w_gate, w_up, w_down):
    experts = lax.axis_size("expert")
    groups = lax.axis_size("dp")
    sizes = {"dp": groups, "expert": experts}
    count = tokens.shape[0]
    width = tokens.shape[1]
    top = routes.shape[1]
    cap = 3 * count * top // (2 * experts)
    slots = experts * cap
    routed = count * top
    flat = routes.reshape(routed)
    labels = jnp.arange(experts, dtype=jnp.int32)
    onehot = (flat[:, None] == labels[None, :]).astype(jnp.int32)
    rank = jnp.sum((jnp.cumsum(onehot, axis=0) - onehot) * onehot, axis=1)
    position = flat * cap + rank
    owner = (
        jnp.full((slots,), routed, jnp.int32).at[position].set(jnp.arange(routed, dtype=jnp.int32))
    )
    source = owner // top
    padded_tokens = jnp.concatenate([tokens, jnp.zeros((1, width), tokens.dtype)], axis=0)
    padded_grads = jnp.concatenate([grad_out, jnp.zeros((1, width), grad_out.dtype)], axis=0)
    padded_gates = jnp.concatenate([gates.reshape(routed), jnp.zeros((1,), jnp.float32)], axis=0)
    inputs_out = padded_tokens[source].reshape(experts, cap, width)
    scaled_out = (padded_gates[owner][:, None] * padded_grads[source].astype(jnp.float32)).astype(
        jnp.bfloat16
    )
    scaled_out = scaled_out.reshape(experts, cap, width)
    share = w_gate.shape[1]
    hid = w_gate.shape[2]
    x_in, s_in, gate_all, up_all, down_all = exchange(
        (("a2a", "expert"), ("a2a", "expert"), ("gather", "dp"), ("gather", "dp"), ("gather", "dp")),
        sizes,
        (inputs_out, scaled_out, w_gate[0], w_up[0], w_down[0]),
        (
            (experts, cap, width),
            (experts, cap, width),
            (groups, share, hid),
            (groups, share, hid),
            (groups, hid, share),
        ),
    )
    x_rows = x_in.reshape(slots, width)
    scaled_rows = s_in.reshape(slots, width)
    gate_full = gate_all.reshape(groups * share, hid)
    up_full = up_all.reshape(groups * share, hid)
    pre_gate = jnp.dot(x_rows, gate_full, preferred_element_type=jnp.float32)
    pre_up = jnp.dot(x_rows, up_full, preferred_element_type=jnp.float32)
    act, slope = silu_parts(pre_gate)
    hidden_f = act * pre_up
    back = jnp.einsum(
        "sgk,ghk->sh",
        scaled_rows.reshape(slots, groups, share),
        down_all,
        preferred_element_type=jnp.float32,
    )
    score = jnp.sum(back * hidden_f, axis=1).astype(jnp.bfloat16)
    d_gate = (back * pre_up * slope).astype(jnp.bfloat16)
    d_up = (back * act).astype(jnp.bfloat16)
    route_grad = (contract_last(d_gate, gate_full) + contract_last(d_up, up_full)).astype(
        jnp.bfloat16
    )
    hidden = hidden_f.astype(jnp.bfloat16)
    partial = jnp.einsum(
        "sh,sgk->ghk",
        hidden,
        scaled_rows.reshape(slots, groups, share),
        preferred_element_type=jnp.float32,
    ).astype(jnp.bfloat16)
    score_box = jnp.zeros((experts, 8, 128), jnp.bfloat16).at[:, 0, :cap].set(
        score.reshape(experts, cap)
    )
    rg_back, score_back, parts_in = exchange(
        (("a2a", "expert"), ("a2a", "expert"), ("a2a", "dp")),
        sizes,
        (route_grad.reshape(experts, cap, width), score_box, partial),
        ((experts, cap, width), (experts, 8, 128), (groups, hid, share)),
    )
    grad_down = jnp.sum(parts_in.astype(jnp.float32), axis=0)[None]
    back_rows = rg_back.reshape(slots, width)
    back_scores = score_back[:, 0, :cap].reshape(slots)
    per_route = back_rows[position].reshape(count, top, width)
    grad_tokens = jnp.sum(per_route.astype(jnp.float32), axis=1).astype(jnp.bfloat16)
    grad_gates = back_scores[position].astype(jnp.float32).reshape(count, top) / gates
    return (grad_tokens, grad_gates, grad_down)


def solution(mesh):
    placed = (
        P(("dp", "expert"), None),
        P(("dp", "expert"), None),
        P(("dp", "expert"), None),
        P(("dp", "expert"), None),
        P("expert", "dp", None),
        P("expert", "dp", None),
        P("expert", None, "dp"),
    )
    return jax.shard_map(
        per_device,
        mesh=mesh,
        in_specs=placed,
        out_specs=(P(("dp", "expert"), None), P(("dp", "expert"), None), P("expert", None, "dp")),
        check_vma=False,
    )
```

```python
import functools

import jax
import jax.numpy as jnp
from jax import lax
from jax.experimental import pallas as pl
from jax.experimental.pallas import tpu as pltpu
from jax.sharding import PartitionSpec as P


def silu_parts(pre):
    sig = jax.nn.sigmoid(pre)
    return (pre * sig, sig * (1.0 + pre * (1.0 - sig)))


def contract_last(left, right):
    return lax.dot_general(
        left, right, (((1,), (1,)), ((), ())), preferred_element_type=jnp.float32
    )


def xfer_kernel(plan, sizes, *refs):
    count = len(plan)
    srcs, dsts = refs[:count], refs[count:2 * count]
    send, recv, own = refs[2 * count:2 * count + 3]
    me_dp = lax.axis_index("dp")
    me_ex = lax.axis_index("expert")
    mine = {"dp": me_dp, "expert": me_ex}

    def block(i, peer):
        return srcs[i].at[peer] if plan[i][0] == "a2a" else srcs[i]

    def remote(i, peer, slot):
        axis = plan[i][1]
        device = (peer, me_ex) if axis == "dp" else (me_dp, peer)
        return pltpu.make_async_remote_copy(
            src_ref=block(i, peer),
            dst_ref=dsts[i].at[slot],
            send_sem=send.at[i, peer],
            recv_sem=recv.at[i, slot],
            device_id=device,
            device_id_type=pl.DeviceIdType.MESH,
        )

    local = []
    for i, (kind, axis) in enumerate(plan):
        me = mine[axis]
        copy = pltpu.make_async_copy(block(i, me), dsts[i].at[me], own.at[i])
        copy.start()
        local.append(copy)
    for i, (kind, axis) in enumerate(plan):
        me, n = mine[axis], sizes[axis]

        @pl.loop(1, n)
        def _(j):
            peer = lax.rem(me + j, n)
            remote(i, peer, me).start()

    for i, (kind, axis) in enumerate(plan):
        me, n = mine[axis], sizes[axis]

        @pl.loop(1, n)
        def _(j):
            peer = lax.rem(me + j, n)
            remote(i, peer, me).wait_send()
            remote(i, peer, peer).wait_recv()

    for copy in local:
        copy.wait()


def exchange(plan, sizes, srcs, dst_shapes):
    count = len(plan)
    most = max(sizes.values())
    return pl.pallas_call(
        functools.partial(xfer_kernel, plan, sizes),
        out_shape=[jax.ShapeDtypeStruct(s, a.dtype) for s, a in zip(dst_shapes, srcs)],
        in_specs=[pl.BlockSpec(memory_space=pl.ANY)] * count,
        out_specs=[pl.BlockSpec(memory_space=pl.ANY)] * count,
        scratch_shapes=[
            pltpu.SemaphoreType.DMA((count, most)),
            pltpu.SemaphoreType.DMA((count, most)),
            pltpu.SemaphoreType.DMA((count,)),
        ],
        compiler_params=pltpu.CompilerParams(has_side_effects=True),
    )(*srcs)


def per_device(tokens, routes, gates, grad_out, w_gate, w_up, w_down):
    experts = lax.axis_size("expert")
    groups = lax.axis_size("dp")
    sizes = {"dp": groups, "expert": experts}
    count = tokens.shape[0]
    width = tokens.shape[1]
    top = routes.shape[1]
    cap = 3 * count * top // (2 * experts)
    slots = experts * cap
    routed = count * top
    flat = routes.reshape(routed)
    labels = jnp.arange(experts, dtype=jnp.int32)
    onehot = (flat[:, None] == labels[None, :]).astype(jnp.int32)
    rank = jnp.sum((jnp.cumsum(onehot, axis=0) - onehot) * onehot, axis=1)
    position = flat * cap + rank
    owner = (
        jnp.full((slots,), routed, jnp.int32).at[position].set(jnp.arange(routed, dtype=jnp.int32))
    )
    source = owner // top
    padded_tokens = jnp.concatenate([tokens, jnp.zeros((1, width), tokens.dtype)], axis=0)
    padded_grads = jnp.concatenate([grad_out, jnp.zeros((1, width), grad_out.dtype)], axis=0)
    padded_gates = jnp.concatenate([gates.reshape(routed), jnp.zeros((1,), jnp.float32)], axis=0)
    dense = (experts, cap * width // 128, 128)
    inputs_out = padded_tokens[source].reshape(dense)
    scaled_out = (padded_gates[owner][:, None] * padded_grads[source].astype(jnp.float32)).astype(
        jnp.bfloat16
    )
    scaled_out = scaled_out.reshape(dense)
    share = w_gate.shape[1]
    hid = w_gate.shape[2]
    x_in, s_in, gate_all, up_all, down_all = exchange(
        (("a2a", "expert"), ("a2a", "expert"), ("gather", "dp"), ("gather", "dp"), ("gather", "dp")),
        sizes,
        (inputs_out, scaled_out, w_gate[0], w_up[0], w_down[0]),
        (
            dense,
            dense,
            (groups, share, hid),
            (groups, share, hid),
            (groups, hid, share),
        ),
    )
    x_rows = x_in.reshape(slots, width)
    scaled_rows = s_in.reshape(slots, width)
    gate_full = gate_all.reshape(groups * share, hid)
    up_full = up_all.reshape(groups * share, hid)
    pre_gate = jnp.dot(x_rows, gate_full, preferred_element_type=jnp.float32)
    pre_up = jnp.dot(x_rows, up_full, preferred_element_type=jnp.float32)
    act, slope = silu_parts(pre_gate)
    hidden_f = act * pre_up
    back = jnp.einsum(
        "sgk,ghk->sh",
        scaled_rows.reshape(slots, groups, share),
        down_all,
        preferred_element_type=jnp.float32,
    )
    score = jnp.sum(back * hidden_f, axis=1).astype(jnp.bfloat16)
    d_gate = (back * pre_up * slope).astype(jnp.bfloat16)
    d_up = (back * act).astype(jnp.bfloat16)
    route_grad = (contract_last(d_gate, gate_full) + contract_last(d_up, up_full)).astype(
        jnp.bfloat16
    )
    hidden = hidden_f.astype(jnp.bfloat16)
    partial = jnp.einsum(
        "sh,sgk->ghk",
        hidden,
        scaled_rows.reshape(slots, groups, share),
        preferred_element_type=jnp.float32,
    ).astype(jnp.bfloat16)
    score_box = jnp.zeros((experts, 8, 128), jnp.bfloat16).at[:, 0, :cap].set(
        score.reshape(experts, cap)
    )
    rg_back, score_back, parts_in = exchange(
        (("a2a", "expert"), ("a2a", "expert"), ("a2a", "dp")),
        sizes,
        (route_grad.reshape(dense), score_box, partial),
        (dense, (experts, 8, 128), (groups, hid, share)),
    )
    grad_down = jnp.sum(parts_in.astype(jnp.float32), axis=0)[None]
    back_rows = rg_back.reshape(slots, width)
    back_scores = score_back[:, 0, :cap].reshape(slots)
    per_route = back_rows[position].reshape(count, top, width)
    grad_tokens = jnp.sum(per_route.astype(jnp.float32), axis=1).astype(jnp.bfloat16)
    grad_gates = back_scores[position].astype(jnp.float32).reshape(count, top) / gates
    return (grad_tokens, grad_gates, grad_down)


def solution(mesh):
    placed = (
        P(("dp", "expert"), None),
        P(("dp", "expert"), None),
        P(("dp", "expert"), None),
        P(("dp", "expert"), None),
        P("expert", "dp", None),
        P("expert", "dp", None),
        P("expert", None, "dp"),
    )
    return jax.shard_map(
        per_device,
        mesh=mesh,
        in_specs=placed,
        out_specs=(P(("dp", "expert"), None), P(("dp", "expert"), None), P("expert", None, "dp")),
        check_vma=False,
    )
```

```python
import functools

import jax
import jax.numpy as jnp
from jax import lax
from jax.experimental import pallas as pl
from jax.experimental.pallas import tpu as pltpu
from jax.sharding import PartitionSpec as P


def silu_parts(pre):
    sig = jax.nn.sigmoid(pre)
    return (pre * sig, sig * (1.0 + pre * (1.0 - sig)))


def contract_last(left, right):
    return lax.dot_general(
        left, right, (((1,), (1,)), ((), ())), preferred_element_type=jnp.float32
    )


def turn(j, n):
    odd = j % 2
    return odd * ((j + 1) // 2) + (1 - odd) * (n - j // 2)


def xfer_kernel(plan, sizes, *refs):
    count = len(plan)
    srcs, dsts = refs[:count], refs[count:2 * count]
    send, recv, own = refs[2 * count:2 * count + 3]
    me_dp = lax.axis_index("dp")
    me_ex = lax.axis_index("expert")
    mine = {"dp": me_dp, "expert": me_ex}

    def block(i, peer):
        return srcs[i].at[peer] if plan[i][0] == "a2a" else srcs[i]

    def remote(i, peer, slot):
        axis = plan[i][1]
        device = (peer, me_ex) if axis == "dp" else (me_dp, peer)
        return pltpu.make_async_remote_copy(
            src_ref=block(i, peer),
            dst_ref=dsts[i].at[slot],
            send_sem=send.at[i, peer],
            recv_sem=recv.at[i, slot],
            device_id=device,
            device_id_type=pl.DeviceIdType.MESH,
        )

    barrier = pltpu.get_barrier_semaphore()
    axes = sorted(set(axis for _, axis in plan))
    for axis in axes:
        me, n = mine[axis], sizes[axis]

        @pl.loop(1, n)
        def _(j):
            peer = lax.rem(me + j, n)
            device = (peer, me_ex) if axis == "dp" else (me_dp, peer)
            pl.semaphore_signal(
                barrier, 1, device_id=device, device_id_type=pl.DeviceIdType.MESH
            )

    pl.semaphore_wait(barrier, sum(sizes[axis] - 1 for axis in axes))

    local = []
    for i, (kind, axis) in enumerate(plan):
        me = mine[axis]
        copy = pltpu.make_async_copy(block(i, me), dsts[i].at[me], own.at[i])
        copy.start()
        local.append(copy)
    for i, (kind, axis) in enumerate(plan):
        me, n = mine[axis], sizes[axis]

        @pl.loop(1, n)
        def _(j):
            peer = lax.rem(me + turn(j, n), n)
            remote(i, peer, me).start()

    for i, (kind, axis) in enumerate(plan):
        me, n = mine[axis], sizes[axis]

        @pl.loop(1, n)
        def _(j):
            peer = lax.rem(me + turn(j, n), n)
            remote(i, peer, me).wait_send()
            remote(i, peer, peer).wait_recv()

    for copy in local:
        copy.wait()


def exchange(plan, sizes, srcs, dst_shapes, tag):
    count = len(plan)
    most = max(sizes.values())
    return pl.pallas_call(
        functools.partial(xfer_kernel, plan, sizes),
        out_shape=[jax.ShapeDtypeStruct(s, a.dtype) for s, a in zip(dst_shapes, srcs)],
        in_specs=[pl.BlockSpec(memory_space=pl.ANY)] * count,
        out_specs=[pl.BlockSpec(memory_space=pl.ANY)] * count,
        scratch_shapes=[
            pltpu.SemaphoreType.DMA((count, most)),
            pltpu.SemaphoreType.DMA((count, most)),
            pltpu.SemaphoreType.DMA((count,)),
        ],
        compiler_params=pltpu.CompilerParams(collective_id=tag, has_side_effects=True),
    )(*srcs)


def per_device(tokens, routes, gates, grad_out, w_gate, w_up, w_down):
    experts = lax.axis_size("expert")
    groups = lax.axis_size("dp")
    sizes = {"dp": groups, "expert": experts}
    count = tokens.shape[0]
    width = tokens.shape[1]
    top = routes.shape[1]
    cap = 3 * count * top // (2 * experts)
    slots = experts * cap
    routed = count * top
    flat = routes.reshape(routed)
    labels = jnp.arange(experts, dtype=jnp.int32)
    onehot = (flat[:, None] == labels[None, :]).astype(jnp.int32)
    rank = jnp.sum((jnp.cumsum(onehot, axis=0) - onehot) * onehot, axis=1)
    position = flat * cap + rank
    owner = (
        jnp.full((slots,), routed, jnp.int32).at[position].set(jnp.arange(routed, dtype=jnp.int32))
    )
    source = owner // top
    padded_tokens = jnp.concatenate([tokens, jnp.zeros((1, width), tokens.dtype)], axis=0)
    padded_grads = jnp.concatenate([grad_out, jnp.zeros((1, width), grad_out.dtype)], axis=0)
    padded_gates = jnp.concatenate([gates.reshape(routed), jnp.zeros((1,), jnp.float32)], axis=0)
    dense = (experts, cap * width // 128, 128)
    inputs_out = padded_tokens[source].reshape(dense)
    scaled_out = (padded_gates[owner][:, None] * padded_grads[source].astype(jnp.float32)).astype(
        jnp.bfloat16
    )
    scaled_out = scaled_out.reshape(dense)
    share = w_gate.shape[1]
    hid = w_gate.shape[2]
    x_in, s_in, gate_all, up_all, down_all = exchange(
        (("a2a", "expert"), ("a2a", "expert"), ("gather", "dp"), ("gather", "dp"), ("gather", "dp")),
        sizes,
        (inputs_out, scaled_out, w_gate[0], w_up[0], w_down[0]),
        (
            dense,
            dense,
            (groups, share, hid),
            (groups, share, hid),
            (groups, hid, share),
        ),
        0,
    )
    x_rows = x_in.reshape(slots, width)
    scaled_rows = s_in.reshape(slots, width)
    gate_full = gate_all.reshape(groups * share, hid)
    up_full = up_all.reshape(groups * share, hid)
    pre_gate = jnp.dot(x_rows, gate_full, preferred_element_type=jnp.float32)
    pre_up = jnp.dot(x_rows, up_full, preferred_element_type=jnp.float32)
    act, slope = silu_parts(pre_gate)
    hidden_f = act * pre_up
    back = jnp.einsum(
        "sgk,ghk->sh",
        scaled_rows.reshape(slots, groups, share),
        down_all,
        preferred_element_type=jnp.float32,
    )
    score = jnp.sum(back * hidden_f, axis=1).astype(jnp.bfloat16)
    d_gate = (back * pre_up * slope).astype(jnp.bfloat16)
    d_up = (back * act).astype(jnp.bfloat16)
    route_grad = (contract_last(d_gate, gate_full) + contract_last(d_up, up_full)).astype(
        jnp.bfloat16
    )
    hidden = hidden_f.astype(jnp.bfloat16)
    partial = jnp.einsum(
        "sh,sgk->ghk",
        hidden,
        scaled_rows.reshape(slots, groups, share),
        preferred_element_type=jnp.float32,
    ).astype(jnp.bfloat16)
    score_box = jnp.zeros((experts, 8, 128), jnp.bfloat16).at[:, 0, :cap].set(
        score.reshape(experts, cap)
    )
    rg_back, score_back, parts_in = exchange(
        (("a2a", "expert"), ("a2a", "expert"), ("a2a", "dp")),
        sizes,
        (route_grad.reshape(dense), score_box, partial),
        (dense, (experts, 8, 128), (groups, hid, share)),
        1,
    )
    grad_down = jnp.sum(parts_in.astype(jnp.float32), axis=0)[None]
    back_rows = rg_back.reshape(slots, width)
    back_scores = score_back[:, 0, :cap].reshape(slots)
    per_route = back_rows[position].reshape(count, top, width)
    grad_tokens = jnp.sum(per_route.astype(jnp.float32), axis=1).astype(jnp.bfloat16)
    grad_gates = back_scores[position].astype(jnp.float32).reshape(count, top) / gates
    return (grad_tokens, grad_gates, grad_down)


def solution(mesh):
    placed = (
        P(("dp", "expert"), None),
        P(("dp", "expert"), None),
        P(("dp", "expert"), None),
        P(("dp", "expert"), None),
        P("expert", "dp", None),
        P("expert", "dp", None),
        P("expert", None, "dp"),
    )
    return jax.shard_map(
        per_device,
        mesh=mesh,
        in_specs=placed,
        out_specs=(P(("dp", "expert"), None), P(("dp", "expert"), None), P("expert", None, "dp")),
        check_vma=False,
    )
```

```python
import functools

import jax
import jax.numpy as jnp
from jax import lax
from jax.experimental import pallas as pl
from jax.experimental.pallas import tpu as pltpu
from jax.sharding import PartitionSpec as P


def silu_parts(pre):
    sig = jax.nn.sigmoid(pre)
    return (pre * sig, sig * (1.0 + pre * (1.0 - sig)))


def contract_last(left, right):
    return lax.dot_general(
        left, right, (((1,), (1,)), ((), ())), preferred_element_type=jnp.float32
    )


def turn(j, n):
    odd = j % 2
    return odd * ((j + 1) // 2) + (1 - odd) * (n - j // 2)


def xfer_kernel(plan, sizes, *refs):
    count = len(plan)
    srcs, dsts = refs[:count], refs[count:2 * count]
    send, recv, own = refs[2 * count:2 * count + 3]
    me_dp = lax.axis_index("dp")
    me_ex = lax.axis_index("expert")
    mine = {"dp": me_dp, "expert": me_ex}

    def block(i, peer):
        return srcs[i].at[peer] if plan[i][0] == "a2a" else srcs[i]

    def remote(i, peer, slot):
        axis = plan[i][1]
        device = (peer, me_ex) if axis == "dp" else (me_dp, peer)
        return pltpu.make_async_remote_copy(
            src_ref=block(i, peer),
            dst_ref=dsts[i].at[slot],
            send_sem=send.at[i, peer],
            recv_sem=recv.at[i, slot],
            device_id=device,
            device_id_type=pl.DeviceIdType.MESH,
        )

    barrier = pltpu.get_barrier_semaphore()
    axes = sorted(set(axis for _, axis in plan))
    for axis in axes:
        me, n = mine[axis], sizes[axis]

        @pl.loop(1, n)
        def _(j):
            peer = lax.rem(me + j, n)
            device = (peer, me_ex) if axis == "dp" else (me_dp, peer)
            pl.semaphore_signal(
                barrier, 1, device_id=device, device_id_type=pl.DeviceIdType.MESH
            )

    pl.semaphore_wait(barrier, sum(sizes[axis] - 1 for axis in axes))

    local = []
    for i, (kind, axis) in enumerate(plan):
        me = mine[axis]
        copy = pltpu.make_async_copy(block(i, me), dsts[i].at[me], own.at[i])
        copy.start()
        local.append(copy)
    for i, (kind, axis) in enumerate(plan):
        me, n = mine[axis], sizes[axis]

        @pl.loop(1, n)
        def _(j):
            peer = lax.rem(me + turn(j, n), n)
            remote(i, peer, me).start()

    for i, (kind, axis) in enumerate(plan):
        me, n = mine[axis], sizes[axis]

        @pl.loop(1, n)
        def _(j):
            peer = lax.rem(me + turn(j, n), n)
            remote(i, peer, me).wait_send()
            remote(i, peer, peer).wait_recv()

    for copy in local:
        copy.wait()


def exchange(plan, sizes, srcs, dst_shapes, tag):
    count = len(plan)
    most = max(sizes.values())
    return pl.pallas_call(
        functools.partial(xfer_kernel, plan, sizes),
        out_shape=[jax.ShapeDtypeStruct(s, a.dtype) for s, a in zip(dst_shapes, srcs)],
        in_specs=[pl.BlockSpec(memory_space=pl.ANY)] * count,
        out_specs=[pl.BlockSpec(memory_space=pl.ANY)] * count,
        scratch_shapes=[
            pltpu.SemaphoreType.DMA((count, most)),
            pltpu.SemaphoreType.DMA((count, most)),
            pltpu.SemaphoreType.DMA((count,)),
        ],
        compiler_params=pltpu.CompilerParams(collective_id=tag, has_side_effects=True),
    )(*srcs)


def per_device(tokens, routes, gates, grad_out, w_gate, w_up, w_down):
    experts = lax.axis_size("expert")
    groups = lax.axis_size("dp")
    sizes = {"dp": groups, "expert": experts}
    count = tokens.shape[0]
    width = tokens.shape[1]
    top = routes.shape[1]
    cap = 3 * count * top // (2 * experts)
    slots = experts * cap
    routed = count * top
    flat = routes.reshape(routed)
    labels = jnp.arange(experts, dtype=jnp.int32)
    onehot = (flat[:, None] == labels[None, :]).astype(jnp.int32)
    rank = jnp.sum((jnp.cumsum(onehot, axis=0) - onehot) * onehot, axis=1)
    position = flat * cap + rank
    owner = (
        jnp.full((slots,), routed, jnp.int32).at[position].set(jnp.arange(routed, dtype=jnp.int32))
    )
    source = owner // top
    lanes = width // 128
    pick = (source[:, None] == jnp.arange(count, dtype=jnp.int32)[None, :]).astype(jnp.bfloat16)
    select = (((1,), (0,)), ((), ()))
    x_send = lax.dot_general(
        pick, tokens.reshape(count, lanes, 128), select, preferred_element_type=jnp.float32
    ).astype(jnp.bfloat16)
    g_rows = lax.dot_general(
        pick, grad_out.reshape(count, lanes, 128), select, preferred_element_type=jnp.float32
    )
    padded_gates = jnp.concatenate([gates.reshape(routed), jnp.zeros((1,), jnp.float32)], axis=0)
    s_send = (padded_gates[owner][:, None, None] * g_rows).astype(jnp.bfloat16)
    dense = (experts, cap * lanes, 128)
    share = w_gate.shape[1]
    hid = w_gate.shape[2]
    x_in, s_in, gate_all, up_all, down_all = exchange(
        (("a2a", "expert"), ("a2a", "expert"), ("gather", "dp"), ("gather", "dp"), ("gather", "dp")),
        sizes,
        (x_send.reshape(dense), s_send.reshape(dense), w_gate[0], w_up[0], w_down[0].T),
        (dense, dense, (groups, share, hid), (groups, share, hid), (groups, share, hid)),
        0,
    )
    x3 = x_in.reshape(slots, lanes, 128)
    s3 = s_in.reshape(slots, lanes, 128)
    gate3 = gate_all.reshape(lanes, 128, hid)
    up3 = up_all.reshape(lanes, 128, hid)
    down3 = down_all.reshape(lanes, 128, hid)
    over_d = (((1, 2), (0, 1)), ((), ()))
    pre_gate = lax.dot_general(x3, gate3, over_d, preferred_element_type=jnp.float32)
    pre_up = lax.dot_general(x3, up3, over_d, preferred_element_type=jnp.float32)
    act, slope = silu_parts(pre_gate)
    hidden_f = act * pre_up
    back = lax.dot_general(s3, down3, over_d, preferred_element_type=jnp.float32)
    score = jnp.sum(back * hidden_f, axis=1).astype(jnp.bfloat16)
    d_gate = (back * pre_up * slope).astype(jnp.bfloat16)
    d_up = (back * act).astype(jnp.bfloat16)
    over_h = (((1,), (2,)), ((), ()))
    route_grad = (
        lax.dot_general(d_gate, gate3, over_h, preferred_element_type=jnp.float32)
        + lax.dot_general(d_up, up3, over_h, preferred_element_type=jnp.float32)
    ).astype(jnp.bfloat16)
    hidden = hidden_f.astype(jnp.bfloat16)
    partial = lax.dot_general(
        s3, hidden, (((0,), (0,)), ((), ())), preferred_element_type=jnp.float32
    ).astype(jnp.bfloat16)
    score_box = jnp.zeros((experts, 8, 128), jnp.bfloat16).at[:, 0, :cap].set(
        score.reshape(experts, cap)
    )
    rg_back, score_back, parts_in = exchange(
        (("a2a", "expert"), ("a2a", "expert"), ("a2a", "dp")),
        sizes,
        (route_grad.reshape(dense), score_box, partial.reshape(groups, share, hid)),
        (dense, (experts, 8, 128), (groups, share, hid)),
        1,
    )
    grad_down = jnp.sum(parts_in.astype(jnp.float32), axis=0).T[None]
    summed = lax.dot_general(
        pick, rg_back.reshape(slots, lanes, 128), (((0,), (0,)), ((), ())),
        preferred_element_type=jnp.float32,
    )
    grad_tokens = summed.astype(jnp.bfloat16).reshape(count, width)
    back_scores = score_back[:, 0, :cap].reshape(slots)
    grad_gates = back_scores[position].astype(jnp.float32).reshape(count, top) / gates
    return (grad_tokens, grad_gates, grad_down)


def solution(mesh):
    placed = (
        P(("dp", "expert"), None),
        P(("dp", "expert"), None),
        P(("dp", "expert"), None),
        P(("dp", "expert"), None),
        P("expert", "dp", None),
        P("expert", "dp", None),
        P("expert", None, "dp"),
    )
    return jax.shard_map(
        per_device,
        mesh=mesh,
        in_specs=placed,
        out_specs=(P(("dp", "expert"), None), P(("dp", "expert"), None), P("expert", None, "dp")),
        check_vma=False,
    )
```

```python
import functools

import jax
import jax.numpy as jnp
from jax import lax
from jax.experimental import pallas as pl
from jax.experimental.pallas import tpu as pltpu
from jax.sharding import PartitionSpec as P


def silu_parts(pre):
    sig = jax.nn.sigmoid(pre)
    return (pre * sig, sig * (1.0 + pre * (1.0 - sig)))


def contract_last(left, right):
    return lax.dot_general(
        left, right, (((1,), (1,)), ((), ())), preferred_element_type=jnp.float32
    )


def turn(j, n):
    odd = j % 2
    return odd * ((j + 1) // 2) + (1 - odd) * (n - j // 2)


def xfer_kernel(plan, sizes, *refs):
    count = len(plan)
    srcs, dsts = refs[:count], refs[count:2 * count]
    send, recv, own = refs[2 * count:2 * count + 3]
    me_dp = lax.axis_index("dp")
    me_ex = lax.axis_index("expert")
    mine = {"dp": me_dp, "expert": me_ex}

    def block(i, peer):
        return srcs[i].at[peer] if plan[i][0] == "a2a" else srcs[i]

    def remote(i, peer, slot):
        axis = plan[i][1]
        device = (peer, me_ex) if axis == "dp" else (me_dp, peer)
        return pltpu.make_async_remote_copy(
            src_ref=block(i, peer),
            dst_ref=dsts[i].at[slot],
            send_sem=send.at[i, peer],
            recv_sem=recv.at[i, slot],
            device_id=device,
            device_id_type=pl.DeviceIdType.MESH,
        )

    barrier = pltpu.get_barrier_semaphore()
    axes = sorted(set(axis for _, axis in plan))
    for axis in axes:
        me, n = mine[axis], sizes[axis]

        @pl.loop(1, n)
        def _(j):
            peer = lax.rem(me + j, n)
            device = (peer, me_ex) if axis == "dp" else (me_dp, peer)
            pl.semaphore_signal(
                barrier, 1, device_id=device, device_id_type=pl.DeviceIdType.MESH
            )

    pl.semaphore_wait(barrier, sum(sizes[axis] - 1 for axis in axes))

    local = []
    for i, (kind, axis) in enumerate(plan):
        me = mine[axis]
        copy = pltpu.make_async_copy(block(i, me), dsts[i].at[me], own.at[i])
        copy.start()
        local.append(copy)
    for i, (kind, axis) in enumerate(plan):
        me, n = mine[axis], sizes[axis]

        @pl.loop(1, n)
        def _(j):
            peer = lax.rem(me + turn(j, n), n)
            remote(i, peer, me).start()

    for i, (kind, axis) in enumerate(plan):
        me, n = mine[axis], sizes[axis]

        @pl.loop(1, n)
        def _(j):
            peer = lax.rem(me + turn(j, n), n)
            remote(i, peer, me).wait_send()
            remote(i, peer, peer).wait_recv()

    for copy in local:
        copy.wait()


def exchange(plan, sizes, srcs, dst_shapes, tag):
    count = len(plan)
    most = max(sizes.values())
    return pl.pallas_call(
        functools.partial(xfer_kernel, plan, sizes),
        out_shape=[jax.ShapeDtypeStruct(s, a.dtype) for s, a in zip(dst_shapes, srcs)],
        in_specs=[pl.BlockSpec(memory_space=pl.ANY)] * count,
        out_specs=[pl.BlockSpec(memory_space=pl.ANY)] * count,
        scratch_shapes=[
            pltpu.SemaphoreType.DMA((count, most)),
            pltpu.SemaphoreType.DMA((count, most)),
            pltpu.SemaphoreType.DMA((count,)),
        ],
        compiler_params=pltpu.CompilerParams(collective_id=tag, has_side_effects=True),
    )(*srcs)


def per_device(tokens, routes, gates, grad_out, w_gate, w_up, w_down):
    experts = lax.axis_size("expert")
    groups = lax.axis_size("dp")
    sizes = {"dp": groups, "expert": experts}
    count = tokens.shape[0]
    width = tokens.shape[1]
    top = routes.shape[1]
    cap = 3 * count * top // (2 * experts)
    slots = experts * cap
    routed = count * top
    flat = routes.reshape(routed)
    labels = jnp.arange(experts, dtype=jnp.int32)
    onehot = (flat[:, None] == labels[None, :]).astype(jnp.int32)
    rank = jnp.sum((jnp.cumsum(onehot, axis=0) - onehot) * onehot, axis=1)
    position = flat * cap + rank
    owner = (
        jnp.full((slots,), routed, jnp.int32).at[position].set(jnp.arange(routed, dtype=jnp.int32))
    )
    source = owner // top
    lanes = width // 128
    pick = (source[:, None] == jnp.arange(count, dtype=jnp.int32)[None, :]).astype(jnp.bfloat16)
    select = (((1,), (0,)), ((), ()))
    x_send = lax.dot_general(
        pick, tokens.reshape(count, lanes, 128), select, preferred_element_type=jnp.float32
    ).astype(jnp.bfloat16)
    g_rows = lax.dot_general(
        pick, grad_out.reshape(count, lanes, 128), select, preferred_element_type=jnp.float32
    )
    route_ids = jnp.arange(routed, dtype=jnp.int32)
    slot_gate = jnp.sum(
        jnp.where(owner[:, None] == route_ids[None, :], gates.reshape(1, routed), 0.0), axis=1
    )
    s_send = (slot_gate[:, None, None] * g_rows).astype(jnp.bfloat16)
    dense = (experts, cap * lanes, 128)
    share = w_gate.shape[1]
    hid = w_gate.shape[2]
    x_in, s_in, gate_all, up_all, down_all = exchange(
        (("a2a", "expert"), ("a2a", "expert"), ("gather", "dp"), ("gather", "dp"), ("gather", "dp")),
        sizes,
        (x_send.reshape(dense), s_send.reshape(dense), w_gate[0], w_up[0], w_down[0].T),
        (dense, dense, (groups, share, hid), (groups, share, hid), (groups, share, hid)),
        0,
    )
    x3 = x_in.reshape(slots, lanes, 128)
    s3 = s_in.reshape(slots, lanes, 128)
    gate3 = gate_all.reshape(lanes, 128, hid)
    up3 = up_all.reshape(lanes, 128, hid)
    down3 = down_all.reshape(lanes, 128, hid)
    over_d = (((1, 2), (0, 1)), ((), ()))
    pre_gate = lax.dot_general(x3, gate3, over_d, preferred_element_type=jnp.float32)
    pre_up = lax.dot_general(x3, up3, over_d, preferred_element_type=jnp.float32)
    act, slope = silu_parts(pre_gate)
    hidden_f = act * pre_up
    back = lax.dot_general(s3, down3, over_d, preferred_element_type=jnp.float32)
    score = jnp.sum(back * hidden_f, axis=1).astype(jnp.bfloat16)
    d_gate = (back * pre_up * slope).astype(jnp.bfloat16)
    d_up = (back * act).astype(jnp.bfloat16)
    over_h = (((1,), (2,)), ((), ()))
    route_grad = (
        lax.dot_general(d_gate, gate3, over_h, preferred_element_type=jnp.float32)
        + lax.dot_general(d_up, up3, over_h, preferred_element_type=jnp.float32)
    ).astype(jnp.bfloat16)
    hidden = hidden_f.astype(jnp.bfloat16)
    partial = lax.dot_general(
        s3, hidden, (((0,), (0,)), ((), ())), preferred_element_type=jnp.float32
    ).astype(jnp.bfloat16)
    score_box = jnp.zeros((experts, 8, 128), jnp.bfloat16).at[:, 0, :cap].set(
        score.reshape(experts, cap)
    )
    rg_back, score_back, parts_in = exchange(
        (("a2a", "expert"), ("a2a", "expert"), ("a2a", "dp")),
        sizes,
        (route_grad.reshape(dense), score_box, partial.reshape(groups, share, hid)),
        (dense, (experts, 8, 128), (groups, share, hid)),
        1,
    )
    grad_down = jnp.sum(parts_in.astype(jnp.float32), axis=0).T[None]
    summed = lax.dot_general(
        pick, rg_back.reshape(slots, lanes, 128), (((0,), (0,)), ((), ())),
        preferred_element_type=jnp.float32,
    )
    grad_tokens = summed.astype(jnp.bfloat16).reshape(count, width)
    back_scores = score_back[:, 0, :cap].reshape(1, slots).astype(jnp.float32)
    slot_ids = jnp.arange(slots, dtype=jnp.int32)
    route_score = jnp.sum(
        jnp.where(position[:, None] == slot_ids[None, :], back_scores, 0.0), axis=1
    )
    grad_gates = route_score.reshape(count, top) / gates
    return (grad_tokens, grad_gates, grad_down)


def solution(mesh):
    placed = (
        P(("dp", "expert"), None),
        P(("dp", "expert"), None),
        P(("dp", "expert"), None),
        P(("dp", "expert"), None),
        P("expert", "dp", None),
        P("expert", "dp", None),
        P("expert", None, "dp"),
    )
    return jax.shard_map(
        per_device,
        mesh=mesh,
        in_specs=placed,
        out_specs=(P(("dp", "expert"), None), P(("dp", "expert"), None), P("expert", None, "dp")),
        check_vma=False,
    )
```

```python
import functools

import jax
import jax.numpy as jnp
from jax import lax
from jax.experimental import pallas as pl
from jax.experimental.pallas import tpu as pltpu
from jax.sharding import PartitionSpec as P


def silu_parts(pre):
    sig = jax.nn.sigmoid(pre)
    return (pre * sig, sig * (1.0 + pre * (1.0 - sig)))


def contract_last(left, right):
    return lax.dot_general(
        left, right, (((1,), (1,)), ((), ())), preferred_element_type=jnp.float32
    )


def turn(j, n):
    odd = j % 2
    return odd * ((j + 1) // 2) + (1 - odd) * (n - j // 2)


def xfer_kernel(plan, sizes, *refs):
    count = len(plan)
    srcs, dsts = refs[:count], refs[count:2 * count]
    send, recv, own = refs[2 * count:2 * count + 3]
    me_dp = lax.axis_index("dp")
    me_ex = lax.axis_index("expert")
    mine = {"dp": me_dp, "expert": me_ex}

    def block(i, peer):
        return srcs[i].at[peer] if plan[i][0] == "a2a" else srcs[i]

    def remote(i, peer, slot):
        axis = plan[i][1]
        device = (peer, me_ex) if axis == "dp" else (me_dp, peer)
        return pltpu.make_async_remote_copy(
            src_ref=block(i, peer),
            dst_ref=dsts[i].at[slot],
            send_sem=send.at[i, peer],
            recv_sem=recv.at[i, slot],
            device_id=device,
            device_id_type=pl.DeviceIdType.MESH,
        )

    barrier = pltpu.get_barrier_semaphore()
    axes = sorted(set(axis for _, axis in plan))
    for axis in axes:
        me, n = mine[axis], sizes[axis]

        @pl.loop(1, n)
        def _(j):
            peer = lax.rem(me + j, n)
            device = (peer, me_ex) if axis == "dp" else (me_dp, peer)
            pl.semaphore_signal(
                barrier, 1, device_id=device, device_id_type=pl.DeviceIdType.MESH
            )

    pl.semaphore_wait(barrier, sum(sizes[axis] - 1 for axis in axes))

    local = []
    for i, (kind, axis) in enumerate(plan):
        me = mine[axis]
        copy = pltpu.make_async_copy(block(i, me), dsts[i].at[me], own.at[i])
        copy.start()
        local.append(copy)
    for i, (kind, axis) in enumerate(plan):
        me, n = mine[axis], sizes[axis]

        @pl.loop(1, n)
        def _(j):
            peer = lax.rem(me + turn(j, n), n)
            remote(i, peer, me).start()

    for i, (kind, axis) in enumerate(plan):
        me, n = mine[axis], sizes[axis]

        @pl.loop(1, n)
        def _(j):
            peer = lax.rem(me + turn(j, n), n)
            remote(i, peer, me).wait_send()
            remote(i, peer, peer).wait_recv()

    for copy in local:
        copy.wait()


def exchange(plan, sizes, srcs, dst_shapes, tag):
    count = len(plan)
    most = max(sizes.values())
    return pl.pallas_call(
        functools.partial(xfer_kernel, plan, sizes),
        out_shape=[jax.ShapeDtypeStruct(s, a.dtype) for s, a in zip(dst_shapes, srcs)],
        in_specs=[pl.BlockSpec(memory_space=pl.ANY)] * count,
        out_specs=[pl.BlockSpec(memory_space=pl.ANY)] * count,
        scratch_shapes=[
            pltpu.SemaphoreType.DMA((count, most)),
            pltpu.SemaphoreType.DMA((count, most)),
            pltpu.SemaphoreType.DMA((count,)),
        ],
        compiler_params=pltpu.CompilerParams(collective_id=tag, has_side_effects=True),
    )(*srcs)


def per_device(tokens, routes, gates, grad_out, w_gate, w_up, w_down):
    experts = lax.axis_size("expert")
    groups = lax.axis_size("dp")
    sizes = {"dp": groups, "expert": experts}
    count = tokens.shape[0]
    width = tokens.shape[1]
    top = routes.shape[1]
    cap = 3 * count * top // (2 * experts)
    slots = experts * cap
    routed = count * top
    flat = routes.reshape(routed)
    route_ids = jnp.arange(routed, dtype=jnp.int32)
    same = (flat[:, None] == flat[None, :]) & (route_ids[None, :] < route_ids[:, None])
    rank = jnp.sum(same.astype(jnp.int32), axis=1)
    position = flat * cap + rank
    hit = position[None, :] == jnp.arange(slots, dtype=jnp.int32)[:, None]
    lanes = width // 128
    pick = jnp.any(hit.reshape(slots, count, top), axis=2).astype(jnp.bfloat16)
    select = (((1,), (0,)), ((), ()))
    x_send = lax.dot_general(
        pick, tokens.reshape(count, lanes, 128), select, preferred_element_type=jnp.float32
    ).astype(jnp.bfloat16)
    g_rows = lax.dot_general(
        pick, grad_out.reshape(count, lanes, 128), select, preferred_element_type=jnp.float32
    )
    slot_gate = jnp.sum(jnp.where(hit, gates.reshape(1, routed), 0.0), axis=1)
    s_send = (slot_gate[:, None, None] * g_rows).astype(jnp.bfloat16)
    dense = (experts, cap * lanes, 128)
    share = w_gate.shape[1]
    hid = w_gate.shape[2]
    x_in, s_in, gate_all, up_all, down_all = exchange(
        (("a2a", "expert"), ("a2a", "expert"), ("gather", "dp"), ("gather", "dp"), ("gather", "dp")),
        sizes,
        (x_send.reshape(dense), s_send.reshape(dense), w_gate[0], w_up[0], w_down[0].T),
        (dense, dense, (groups, share, hid), (groups, share, hid), (groups, share, hid)),
        0,
    )
    x3 = x_in.reshape(slots, lanes, 128)
    s3 = s_in.reshape(slots, lanes, 128)
    gate3 = gate_all.reshape(lanes, 128, hid)
    up3 = up_all.reshape(lanes, 128, hid)
    down3 = down_all.reshape(lanes, 128, hid)
    over_d = (((1, 2), (0, 1)), ((), ()))
    pre_gate = lax.dot_general(x3, gate3, over_d, preferred_element_type=jnp.float32)
    pre_up = lax.dot_general(x3, up3, over_d, preferred_element_type=jnp.float32)
    act, slope = silu_parts(pre_gate)
    hidden_f = act * pre_up
    back = lax.dot_general(s3, down3, over_d, preferred_element_type=jnp.float32)
    score = jnp.sum(back * hidden_f, axis=1).astype(jnp.bfloat16)
    d_gate = (back * pre_up * slope).astype(jnp.bfloat16)
    d_up = (back * act).astype(jnp.bfloat16)
    over_h = (((1,), (2,)), ((), ()))
    route_grad = (
        lax.dot_general(d_gate, gate3, over_h, preferred_element_type=jnp.float32)
        + lax.dot_general(d_up, up3, over_h, preferred_element_type=jnp.float32)
    ).astype(jnp.bfloat16)
    hidden = hidden_f.astype(jnp.bfloat16)
    partial = lax.dot_general(
        s3, hidden, (((0,), (0,)), ((), ())), preferred_element_type=jnp.float32
    ).astype(jnp.bfloat16)
    score_box = jnp.zeros((experts, 8, 128), jnp.bfloat16).at[:, 0, :cap].set(
        score.reshape(experts, cap)
    )
    rg_back, score_back, parts_in = exchange(
        (("a2a", "expert"), ("a2a", "expert"), ("a2a", "dp")),
        sizes,
        (route_grad.reshape(dense), score_box, partial.reshape(groups, share, hid)),
        (dense, (experts, 8, 128), (groups, share, hid)),
        1,
    )
    grad_down = jnp.sum(parts_in.astype(jnp.float32), axis=0).T[None]
    summed = lax.dot_general(
        pick, rg_back.reshape(slots, lanes, 128), (((0,), (0,)), ((), ())),
        preferred_element_type=jnp.float32,
    )
    grad_tokens = summed.astype(jnp.bfloat16).reshape(count, width)
    back_scores = score_back[:, 0, :cap].reshape(slots, 1).astype(jnp.float32)
    route_score = jnp.sum(jnp.where(hit, back_scores, 0.0), axis=0)
    grad_gates = route_score.reshape(count, top) / gates
    return (grad_tokens, grad_gates, grad_down)


def solution(mesh):
    placed = (
        P(("dp", "expert"), None),
        P(("dp", "expert"), None),
        P(("dp", "expert"), None),
        P(("dp", "expert"), None),
        P("expert", "dp", None),
        P("expert", "dp", None),
        P("expert", None, "dp"),
    )
    return jax.shard_map(
        per_device,
        mesh=mesh,
        in_specs=placed,
        out_specs=(P(("dp", "expert"), None), P(("dp", "expert"), None), P("expert", None, "dp")),
        check_vma=False,
    )
```

```python
import functools

import jax
import jax.numpy as jnp
from jax import lax
from jax.experimental import pallas as pl
from jax.experimental.pallas import tpu as pltpu
from jax.sharding import PartitionSpec as P


def silu_parts(pre):
    sig = jax.nn.sigmoid(pre)
    return (pre * sig, sig * (1.0 + pre * (1.0 - sig)))


def contract_last(left, right):
    return lax.dot_general(
        left, right, (((1,), (1,)), ((), ())), preferred_element_type=jnp.float32
    )


def turn(j, n):
    odd = j % 2
    return odd * ((j + 1) // 2) + (1 - odd) * (n - j // 2)


def xfer_kernel(plan, sizes, *refs):
    count = len(plan)
    srcs, dsts = refs[:count], refs[count:2 * count]
    send, recv, own = refs[2 * count:2 * count + 3]
    me_dp = lax.axis_index("dp")
    me_ex = lax.axis_index("expert")
    mine = {"dp": me_dp, "expert": me_ex}

    def block(i, peer):
        return srcs[i].at[peer] if plan[i][0] == "a2a" else srcs[i]

    def remote(i, peer, slot):
        axis = plan[i][1]
        device = (peer, me_ex) if axis == "dp" else (me_dp, peer)
        return pltpu.make_async_remote_copy(
            src_ref=block(i, peer),
            dst_ref=dsts[i].at[slot],
            send_sem=send.at[i, peer],
            recv_sem=recv.at[i, slot],
            device_id=device,
            device_id_type=pl.DeviceIdType.MESH,
        )

    barrier = pltpu.get_barrier_semaphore()
    axes = sorted(set(axis for _, axis in plan))
    for axis in axes:
        me, n = mine[axis], sizes[axis]

        @pl.loop(1, n)
        def _(j):
            peer = lax.rem(me + j, n)
            device = (peer, me_ex) if axis == "dp" else (me_dp, peer)
            pl.semaphore_signal(
                barrier, 1, device_id=device, device_id_type=pl.DeviceIdType.MESH
            )

    pl.semaphore_wait(barrier, sum(sizes[axis] - 1 for axis in axes))

    local = []
    for i, (kind, axis) in enumerate(plan):
        me = mine[axis]
        copy = pltpu.make_async_copy(block(i, me), dsts[i].at[me], own.at[i])
        copy.start()
        local.append(copy)
    for i, (kind, axis) in enumerate(plan):
        me, n = mine[axis], sizes[axis]

        @pl.loop(1, n)
        def _(j):
            peer = lax.rem(me + turn(j, n), n)
            remote(i, peer, me).start()

    for i, (kind, axis) in enumerate(plan):
        me, n = mine[axis], sizes[axis]

        @pl.loop(1, n)
        def _(j):
            peer = lax.rem(me + turn(j, n), n)
            remote(i, peer, me).wait_send()
            remote(i, peer, peer).wait_recv()

    for copy in local:
        copy.wait()


def exchange(plan, sizes, srcs, dst_shapes, tag):
    count = len(plan)
    most = max(sizes.values())
    return pl.pallas_call(
        functools.partial(xfer_kernel, plan, sizes),
        out_shape=[jax.ShapeDtypeStruct(s, a.dtype) for s, a in zip(dst_shapes, srcs)],
        in_specs=[pl.BlockSpec(memory_space=pl.ANY)] * count,
        out_specs=[pl.BlockSpec(memory_space=pl.ANY)] * count,
        scratch_shapes=[
            pltpu.SemaphoreType.DMA((count, most)),
            pltpu.SemaphoreType.DMA((count, most)),
            pltpu.SemaphoreType.DMA((count,)),
        ],
        compiler_params=pltpu.CompilerParams(collective_id=tag, has_side_effects=True),
    )(*srcs)


def per_device(tokens, routes, gates, grad_out, w_gate, w_up, w_down):
    experts = lax.axis_size("expert")
    groups = lax.axis_size("dp")
    sizes = {"dp": groups, "expert": experts}
    count = tokens.shape[0]
    width = tokens.shape[1]
    top = routes.shape[1]
    cap = 3 * count * top // (2 * experts)
    slots = experts * cap
    routed = count * top
    flat = routes.T.reshape(routed)
    route_ids = jnp.arange(routed, dtype=jnp.int32)
    same = (flat[:, None] == flat[None, :]) & (route_ids[None, :] < route_ids[:, None])
    rank = jnp.sum(same.astype(jnp.int32), axis=1)
    position = flat * cap + rank
    hit = position[None, :] == jnp.arange(slots, dtype=jnp.int32)[:, None]
    lanes = width // 128
    pick = jnp.any(hit.reshape(slots, top, count), axis=1).astype(jnp.bfloat16)
    select = (((1,), (0,)), ((), ()))
    x_send = lax.dot_general(
        pick, tokens.reshape(count, lanes, 128), select, preferred_element_type=jnp.float32
    ).astype(jnp.bfloat16)
    g_rows = lax.dot_general(
        pick, grad_out.reshape(count, lanes, 128), select, preferred_element_type=jnp.float32
    )
    slot_gate = jnp.sum(jnp.where(hit, gates.T.reshape(1, routed), 0.0), axis=1)
    s_send = (slot_gate[:, None, None] * g_rows).astype(jnp.bfloat16)
    dense = (experts, cap * lanes, 128)
    share = w_gate.shape[1]
    hid = w_gate.shape[2]
    x_in, s_in, gate_all, up_all, down_all = exchange(
        (("a2a", "expert"), ("a2a", "expert"), ("gather", "dp"), ("gather", "dp"), ("gather", "dp")),
        sizes,
        (x_send.reshape(dense), s_send.reshape(dense), w_gate[0], w_up[0], w_down[0].T),
        (dense, dense, (groups, share, hid), (groups, share, hid), (groups, share, hid)),
        0,
    )
    x3 = x_in.reshape(slots, lanes, 128)
    s3 = s_in.reshape(slots, lanes, 128)
    gate3 = gate_all.reshape(lanes, 128, hid)
    up3 = up_all.reshape(lanes, 128, hid)
    down3 = down_all.reshape(lanes, 128, hid)
    over_d = (((1, 2), (0, 1)), ((), ()))
    pre_gate = lax.dot_general(x3, gate3, over_d, preferred_element_type=jnp.float32)
    pre_up = lax.dot_general(x3, up3, over_d, preferred_element_type=jnp.float32)
    act, slope = silu_parts(pre_gate)
    hidden_f = act * pre_up
    back = lax.dot_general(s3, down3, over_d, preferred_element_type=jnp.float32)
    score = jnp.sum(back * hidden_f, axis=1).astype(jnp.bfloat16)
    d_gate = (back * pre_up * slope).astype(jnp.bfloat16)
    d_up = (back * act).astype(jnp.bfloat16)
    over_h = (((1,), (2,)), ((), ()))
    route_grad = (
        lax.dot_general(d_gate, gate3, over_h, preferred_element_type=jnp.float32)
        + lax.dot_general(d_up, up3, over_h, preferred_element_type=jnp.float32)
    ).astype(jnp.bfloat16)
    hidden = hidden_f.astype(jnp.bfloat16)
    partial = lax.dot_general(
        s3, hidden, (((0,), (0,)), ((), ())), preferred_element_type=jnp.float32
    ).astype(jnp.bfloat16)
    score_box = jnp.zeros((experts, 8, 128), jnp.bfloat16).at[:, 0, :cap].set(
        score.reshape(experts, cap)
    )
    rg_back, score_back, parts_in = exchange(
        (("a2a", "expert"), ("a2a", "expert"), ("a2a", "dp")),
        sizes,
        (route_grad.reshape(dense), score_box, partial.reshape(groups, share, hid)),
        (dense, (experts, 8, 128), (groups, share, hid)),
        1,
    )
    grad_down = jnp.sum(parts_in.astype(jnp.float32), axis=0).T[None]
    summed = lax.dot_general(
        pick, rg_back.reshape(slots, lanes, 128), (((0,), (0,)), ((), ())),
        preferred_element_type=jnp.float32,
    )
    grad_tokens = summed.astype(jnp.bfloat16).reshape(count, width)
    back_scores = score_back[:, 0, :cap].reshape(slots, 1).astype(jnp.float32)
    route_score = jnp.sum(jnp.where(hit, back_scores, 0.0), axis=0)
    grad_gates = route_score.reshape(top, count).T / gates
    return (grad_tokens, grad_gates, grad_down)


def solution(mesh):
    placed = (
        P(("dp", "expert"), None),
        P(("dp", "expert"), None),
        P(("dp", "expert"), None),
        P(("dp", "expert"), None),
        P("expert", "dp", None),
        P("expert", "dp", None),
        P("expert", None, "dp"),
    )
    return jax.shard_map(
        per_device,
        mesh=mesh,
        in_specs=placed,
        out_specs=(P(("dp", "expert"), None), P(("dp", "expert"), None), P("expert", None, "dp")),
        check_vma=False,
    )
```

```python
import functools

import jax
import jax.numpy as jnp
from jax import lax
from jax.experimental import pallas as pl
from jax.experimental.pallas import tpu as pltpu
from jax.sharding import PartitionSpec as P


def silu_parts(pre):
    sig = jax.nn.sigmoid(pre)
    return (pre * sig, sig * (1.0 + pre * (1.0 - sig)))


def contract_last(left, right):
    return lax.dot_general(
        left, right, (((1,), (1,)), ((), ())), preferred_element_type=jnp.float32
    )


def turn(j, n):
    odd = j % 2
    return odd * ((j + 1) // 2) + (1 - odd) * (n - j // 2)


def xfer_kernel(plan, sizes, *refs):
    count = len(plan)
    srcs, dsts = refs[:count], refs[count:2 * count]
    send, recv, own = refs[2 * count:2 * count + 3]
    me_dp = lax.axis_index("dp")
    me_ex = lax.axis_index("expert")
    mine = {"dp": me_dp, "expert": me_ex}

    def block(i, peer):
        return srcs[i].at[peer] if plan[i][0] == "a2a" else srcs[i]

    def remote(i, peer, slot):
        axis = plan[i][1]
        device = (peer, me_ex) if axis == "dp" else (me_dp, peer)
        return pltpu.make_async_remote_copy(
            src_ref=block(i, peer),
            dst_ref=dsts[i].at[slot],
            send_sem=send.at[i, peer],
            recv_sem=recv.at[i, slot],
            device_id=device,
            device_id_type=pl.DeviceIdType.MESH,
        )

    barrier = pltpu.get_barrier_semaphore()
    axes = sorted(set(axis for _, axis in plan))
    for axis in axes:
        me, n = mine[axis], sizes[axis]

        @pl.loop(1, n)
        def _(j):
            peer = lax.rem(me + j, n)
            device = (peer, me_ex) if axis == "dp" else (me_dp, peer)
            pl.semaphore_signal(
                barrier, 1, device_id=device, device_id_type=pl.DeviceIdType.MESH
            )

    pl.semaphore_wait(barrier, sum(sizes[axis] - 1 for axis in axes))

    local = []
    for i, (kind, axis) in enumerate(plan):
        me = mine[axis]
        copy = pltpu.make_async_copy(block(i, me), dsts[i].at[me], own.at[i])
        copy.start()
        local.append(copy)
    for i, (kind, axis) in enumerate(plan):
        me, n = mine[axis], sizes[axis]

        @pl.loop(1, n)
        def _(j):
            peer = lax.rem(me + turn(j, n), n)
            remote(i, peer, me).start()

    for i, (kind, axis) in enumerate(plan):
        me, n = mine[axis], sizes[axis]

        @pl.loop(1, n)
        def _(j):
            peer = lax.rem(me + turn(j, n), n)
            remote(i, peer, me).wait_send()
            remote(i, peer, peer).wait_recv()

    for copy in local:
        copy.wait()


def exchange(plan, sizes, srcs, dst_shapes, tag):
    count = len(plan)
    most = max(sizes.values())
    return pl.pallas_call(
        functools.partial(xfer_kernel, plan, sizes),
        out_shape=[jax.ShapeDtypeStruct(s, a.dtype) for s, a in zip(dst_shapes, srcs)],
        in_specs=[pl.BlockSpec(memory_space=pl.ANY)] * count,
        out_specs=[pl.BlockSpec(memory_space=pl.ANY)] * count,
        scratch_shapes=[
            pltpu.SemaphoreType.DMA((count, most)),
            pltpu.SemaphoreType.DMA((count, most)),
            pltpu.SemaphoreType.DMA((count,)),
        ],
        compiler_params=pltpu.CompilerParams(collective_id=tag, has_side_effects=True),
    )(*srcs)


def per_device(tokens, routes, gates, grad_out, w_gate, w_up, w_down):
    experts = lax.axis_size("expert")
    groups = lax.axis_size("dp")
    sizes = {"dp": groups, "expert": experts}
    count = tokens.shape[0]
    width = tokens.shape[1]
    top = routes.shape[1]
    cap = 3 * count * top // (2 * experts)
    slots = experts * cap
    routed = count * top
    flat = routes.T.reshape(routed)
    route_ids = jnp.arange(routed, dtype=jnp.int32)
    same = (flat[:, None] == flat[None, :]) & (route_ids[None, :] < route_ids[:, None])
    rank = jnp.sum(same.astype(jnp.int32), axis=1)
    position = flat * cap + rank
    hit = position[None, :] == jnp.arange(slots, dtype=jnp.int32)[:, None]
    lanes = width // 128
    pick = jnp.any(hit.reshape(slots, top, count), axis=1).astype(jnp.bfloat16)
    select = (((1,), (0,)), ((), ()))
    x_send = lax.dot_general(
        pick, tokens.reshape(count, lanes, 128), select, preferred_element_type=jnp.float32
    ).astype(jnp.bfloat16)
    g_rows = lax.dot_general(
        pick, grad_out.reshape(count, lanes, 128), select, preferred_element_type=jnp.float32
    )
    slot_gate = jnp.sum(jnp.where(hit, gates.T.reshape(1, routed), 0.0), axis=1)
    s_send = (slot_gate[:, None, None] * g_rows).astype(jnp.bfloat16)
    dense = (experts, cap * lanes, 128)
    eye = jnp.eye(w_down.shape[2], dtype=w_down.dtype)
    down_t = lax.dot_general(
        eye, w_down[0], (((1,), (1,)), ((), ())), preferred_element_type=jnp.float32
    ).astype(w_down.dtype)
    share = w_gate.shape[1]
    hid = w_gate.shape[2]
    x_in, s_in, gate_all, up_all, down_all = exchange(
        (("a2a", "expert"), ("a2a", "expert"), ("gather", "dp"), ("gather", "dp"), ("gather", "dp")),
        sizes,
        (x_send.reshape(dense), s_send.reshape(dense), w_gate[0], w_up[0], down_t),
        (dense, dense, (groups, share, hid), (groups, share, hid), (groups, share, hid)),
        0,
    )
    x3 = x_in.reshape(slots, lanes, 128)
    s3 = s_in.reshape(slots, lanes, 128)
    gate3 = gate_all.reshape(lanes, 128, hid)
    up3 = up_all.reshape(lanes, 128, hid)
    down3 = down_all.reshape(lanes, 128, hid)
    over_d = (((1, 2), (0, 1)), ((), ()))
    pre_gate = lax.dot_general(x3, gate3, over_d, preferred_element_type=jnp.float32)
    pre_up = lax.dot_general(x3, up3, over_d, preferred_element_type=jnp.float32)
    act, slope = silu_parts(pre_gate)
    hidden_f = act * pre_up
    back = lax.dot_general(s3, down3, over_d, preferred_element_type=jnp.float32)
    score = jnp.sum(back * hidden_f, axis=1).astype(jnp.bfloat16)
    d_gate = (back * pre_up * slope).astype(jnp.bfloat16)
    d_up = (back * act).astype(jnp.bfloat16)
    over_h = (((1,), (2,)), ((), ()))
    route_grad = (
        lax.dot_general(d_gate, gate3, over_h, preferred_element_type=jnp.float32)
        + lax.dot_general(d_up, up3, over_h, preferred_element_type=jnp.float32)
    ).astype(jnp.bfloat16)
    hidden = hidden_f.astype(jnp.bfloat16)
    partial = lax.dot_general(
        s3, hidden, (((0,), (0,)), ((), ())), preferred_element_type=jnp.float32
    ).astype(jnp.bfloat16)
    score_box = jnp.zeros((experts, 8, 128), jnp.bfloat16).at[:, 0, :cap].set(
        score.reshape(experts, cap)
    )
    rg_back, score_back, parts_in = exchange(
        (("a2a", "expert"), ("a2a", "expert"), ("a2a", "dp")),
        sizes,
        (route_grad.reshape(dense), score_box, partial.reshape(groups, share, hid)),
        (dense, (experts, 8, 128), (groups, share, hid)),
        1,
    )
    grad_down = jnp.sum(parts_in.astype(jnp.float32), axis=0).T[None]
    summed = lax.dot_general(
        pick, rg_back.reshape(slots, lanes, 128), (((0,), (0,)), ((), ())),
        preferred_element_type=jnp.float32,
    )
    grad_tokens = summed.astype(jnp.bfloat16).reshape(count, width)
    back_scores = score_back[:, 0, :cap].reshape(slots, 1).astype(jnp.float32)
    route_score = jnp.sum(jnp.where(hit, back_scores, 0.0), axis=0)
    grad_gates = route_score.reshape(top, count).T / gates
    return (grad_tokens, grad_gates, grad_down)


def solution(mesh):
    placed = (
        P(("dp", "expert"), None),
        P(("dp", "expert"), None),
        P(("dp", "expert"), None),
        P(("dp", "expert"), None),
        P("expert", "dp", None),
        P("expert", "dp", None),
        P("expert", None, "dp"),
    )
    return jax.shard_map(
        per_device,
        mesh=mesh,
        in_specs=placed,
        out_specs=(P(("dp", "expert"), None), P(("dp", "expert"), None), P("expert", None, "dp")),
        check_vma=False,
    )
```

```python
import functools

import jax
import jax.numpy as jnp
from jax import lax
from jax.experimental import pallas as pl
from jax.experimental.pallas import tpu as pltpu
from jax.sharding import PartitionSpec as P


def silu_parts(pre):
    sig = jax.nn.sigmoid(pre)
    return (pre * sig, sig * (1.0 + pre * (1.0 - sig)))


def contract_last(left, right):
    return lax.dot_general(
        left, right, (((1,), (1,)), ((), ())), preferred_element_type=jnp.float32
    )


def turn(j, n):
    odd = j % 2
    return odd * ((j + 1) // 2) + (1 - odd) * (n - j // 2)


def xfer_kernel(plan, sizes, *refs):
    count = len(plan)
    srcs, dsts = refs[:count], refs[count:2 * count]
    send, recv, own = refs[2 * count:2 * count + 3]
    me_dp = lax.axis_index("dp")
    me_ex = lax.axis_index("expert")
    mine = {"dp": me_dp, "expert": me_ex}

    def block(i, peer):
        return srcs[i].at[peer] if plan[i][0] == "a2a" else srcs[i]

    def remote(i, peer, slot):
        axis = plan[i][1]
        device = (peer, me_ex) if axis == "dp" else (me_dp, peer)
        return pltpu.make_async_remote_copy(
            src_ref=block(i, peer),
            dst_ref=dsts[i].at[slot],
            send_sem=send.at[i, peer],
            recv_sem=recv.at[i, slot],
            device_id=device,
            device_id_type=pl.DeviceIdType.MESH,
        )

    barrier = pltpu.get_barrier_semaphore()
    axes = sorted(set(axis for _, axis in plan))
    for axis in axes:
        me, n = mine[axis], sizes[axis]

        @pl.loop(1, n)
        def _(j):
            peer = lax.rem(me + j, n)
            device = (peer, me_ex) if axis == "dp" else (me_dp, peer)
            pl.semaphore_signal(
                barrier, 1, device_id=device, device_id_type=pl.DeviceIdType.MESH
            )

    pl.semaphore_wait(barrier, sum(sizes[axis] - 1 for axis in axes))

    local = []
    for i, (kind, axis) in enumerate(plan):
        me = mine[axis]
        copy = pltpu.make_async_copy(block(i, me), dsts[i].at[me], own.at[i])
        copy.start()
        local.append(copy)
    for i, (kind, axis) in enumerate(plan):
        me, n = mine[axis], sizes[axis]

        @pl.loop(1, n)
        def _(j):
            peer = lax.rem(me + turn(j, n), n)
            remote(i, peer, me).start()

    for i, (kind, axis) in enumerate(plan):
        me, n = mine[axis], sizes[axis]

        @pl.loop(1, n)
        def _(j):
            peer = lax.rem(me + turn(j, n), n)
            remote(i, peer, me).wait_send()
            remote(i, peer, peer).wait_recv()

    for copy in local:
        copy.wait()


def exchange(plan, sizes, srcs, dst_shapes, tag):
    count = len(plan)
    most = max(sizes.values())
    return pl.pallas_call(
        functools.partial(xfer_kernel, plan, sizes),
        out_shape=[jax.ShapeDtypeStruct(s, a.dtype) for s, a in zip(dst_shapes, srcs)],
        in_specs=[pl.BlockSpec(memory_space=pl.ANY)] * count,
        out_specs=[pl.BlockSpec(memory_space=pl.ANY)] * count,
        scratch_shapes=[
            pltpu.SemaphoreType.DMA((count, most)),
            pltpu.SemaphoreType.DMA((count, most)),
            pltpu.SemaphoreType.DMA((count,)),
        ],
        compiler_params=pltpu.CompilerParams(collective_id=tag, has_side_effects=True),
    )(*srcs)


def per_device(tokens, routes, gates, grad_out, w_gate, w_up, w_down):
    experts = lax.axis_size("expert")
    groups = lax.axis_size("dp")
    sizes = {"dp": groups, "expert": experts}
    count = tokens.shape[0]
    width = tokens.shape[1]
    top = routes.shape[1]
    cap = 3 * count * top // (2 * experts)
    slots = experts * cap
    routed = count * top
    flat = routes.T.reshape(routed)
    route_ids = jnp.arange(routed, dtype=jnp.int32)
    same = (flat[:, None] == flat[None, :]) & (route_ids[None, :] < route_ids[:, None])
    rank = jnp.sum(same.astype(jnp.int32), axis=1)
    position = flat * cap + rank
    hit = position[None, :] == jnp.arange(slots, dtype=jnp.int32)[:, None]
    lanes = width // 128
    pick = jnp.any(hit.reshape(slots, top, count), axis=1).astype(jnp.bfloat16)
    select = (((1,), (0,)), ((), ()))
    x_send = lax.dot_general(
        pick, tokens.reshape(count, lanes, 128), select, preferred_element_type=jnp.float32
    ).astype(jnp.bfloat16)
    g_rows = lax.dot_general(
        pick, grad_out.reshape(count, lanes, 128), select, preferred_element_type=jnp.float32
    )
    slot_gate = jnp.sum(jnp.where(hit, gates.T.reshape(1, routed), 0.0), axis=1)
    s_send = (slot_gate[:, None, None] * g_rows).astype(jnp.bfloat16)
    dense = (experts, cap * lanes, 128)
    share = w_gate.shape[1]
    hid = w_gate.shape[2]
    x_in, s_in, gate_all, up_all, down_all = exchange(
        (("a2a", "expert"), ("a2a", "expert"), ("gather", "dp"), ("gather", "dp"), ("gather", "dp")),
        sizes,
        (x_send.reshape(dense), s_send.reshape(dense), w_gate[0], w_up[0], w_down[0].T),
        (dense, dense, (groups, share, hid), (groups, share, hid), (groups, share, hid)),
        0,
    )
    x3 = x_in.reshape(slots, lanes, 128)
    s3 = s_in.reshape(slots, lanes, 128)
    gate3 = gate_all.reshape(lanes, 128, hid)
    up3 = up_all.reshape(lanes, 128, hid)
    down3 = down_all.reshape(lanes, 128, hid)
    over_d = (((1, 2), (0, 1)), ((), ()))
    pre_gate = lax.dot_general(x3, gate3, over_d, preferred_element_type=jnp.float32)
    pre_up = lax.dot_general(x3, up3, over_d, preferred_element_type=jnp.float32)
    act, slope = silu_parts(pre_gate)
    hidden_f = act * pre_up
    back = lax.dot_general(s3, down3, over_d, preferred_element_type=jnp.float32)
    score = jnp.sum(back * hidden_f, axis=1).astype(jnp.bfloat16)
    d_gate = (back * pre_up * slope).astype(jnp.bfloat16)
    d_up = (back * act).astype(jnp.bfloat16)
    over_h = (((1,), (2,)), ((), ()))
    route_grad = (
        lax.dot_general(d_gate, gate3, over_h, preferred_element_type=jnp.float32)
        + lax.dot_general(d_up, up3, over_h, preferred_element_type=jnp.float32)
    ).astype(jnp.bfloat16)
    hidden = hidden_f.astype(jnp.bfloat16)
    partial = lax.dot_general(
        s3, hidden, (((0,), (0,)), ((), ())), preferred_element_type=jnp.float32
    ).astype(jnp.bfloat16)
    score_box = jnp.zeros((experts, 8, 128), jnp.bfloat16).at[:, 0, :cap].set(
        score.reshape(experts, cap)
    )
    rg_back, score_back, parts_in = exchange(
        (("a2a", "expert"), ("a2a", "expert"), ("a2a", "dp")),
        sizes,
        (route_grad.reshape(dense), score_box, partial.reshape(groups, share, hid)),
        (dense, (experts, 8, 128), (groups, share, hid)),
        1,
    )
    fold = jnp.tile(jnp.eye(share, dtype=jnp.bfloat16), (groups, 1))
    grad_down = lax.dot_general(
        parts_in.reshape(groups * share, hid), fold, (((0,), (0,)), ((), ())),
        preferred_element_type=jnp.float32,
    )[None]
    summed = lax.dot_general(
        pick, rg_back.reshape(slots, lanes, 128), (((0,), (0,)), ((), ())),
        preferred_element_type=jnp.float32,
    )
    grad_tokens = summed.astype(jnp.bfloat16).reshape(count, width)
    back_scores = score_back[:, 0, :cap].reshape(slots, 1).astype(jnp.float32)
    route_score = jnp.sum(jnp.where(hit, back_scores, 0.0), axis=0)
    grad_gates = route_score.reshape(top, count).T / gates
    return (grad_tokens, grad_gates, grad_down)


def solution(mesh):
    placed = (
        P(("dp", "expert"), None),
        P(("dp", "expert"), None),
        P(("dp", "expert"), None),
        P(("dp", "expert"), None),
        P("expert", "dp", None),
        P("expert", "dp", None),
        P("expert", None, "dp"),
    )
    return jax.shard_map(
        per_device,
        mesh=mesh,
        in_specs=placed,
        out_specs=(P(("dp", "expert"), None), P(("dp", "expert"), None), P("expert", None, "dp")),
        check_vma=False,
    )
```

```python
import functools

import jax
import jax.numpy as jnp
from jax import lax
from jax.experimental import pallas as pl
from jax.experimental.pallas import tpu as pltpu
from jax.sharding import PartitionSpec as P


def silu_parts(pre):
    sig = jax.nn.sigmoid(pre)
    return (pre * sig, sig * (1.0 + pre * (1.0 - sig)))


def contract_last(left, right):
    return lax.dot_general(
        left, right, (((1,), (1,)), ((), ())), preferred_element_type=jnp.float32
    )


def turn(j, n):
    odd = j % 2
    return odd * ((j + 1) // 2) + (1 - odd) * (n - j // 2)


def xfer_kernel(plan, sizes, *refs):
    count = len(plan)
    srcs, dsts = refs[:count], refs[count:2 * count]
    send, recv, own = refs[2 * count:2 * count + 3]
    me_dp = lax.axis_index("dp")
    me_ex = lax.axis_index("expert")
    mine = {"dp": me_dp, "expert": me_ex}

    def block(i, peer):
        return srcs[i].at[peer] if plan[i][0] == "a2a" else srcs[i]

    def remote(i, peer, slot):
        axis = plan[i][1]
        device = (peer, me_ex) if axis == "dp" else (me_dp, peer)
        return pltpu.make_async_remote_copy(
            src_ref=block(i, peer),
            dst_ref=dsts[i].at[slot],
            send_sem=send.at[i, peer],
            recv_sem=recv.at[i, slot],
            device_id=device,
            device_id_type=pl.DeviceIdType.MESH,
        )

    barrier = pltpu.get_barrier_semaphore()
    axes = sorted(set(axis for _, axis in plan))
    for axis in axes:
        me, n = mine[axis], sizes[axis]

        @pl.loop(1, n)
        def _(j):
            peer = lax.rem(me + j, n)
            device = (peer, me_ex) if axis == "dp" else (me_dp, peer)
            pl.semaphore_signal(
                barrier, 1, device_id=device, device_id_type=pl.DeviceIdType.MESH
            )

    pl.semaphore_wait(barrier, sum(sizes[axis] - 1 for axis in axes))

    local = []
    for i, (kind, axis) in enumerate(plan):
        me = mine[axis]
        copy = pltpu.make_async_copy(block(i, me), dsts[i].at[me], own.at[i])
        copy.start()
        local.append(copy)
    partner = me_dp + 1 - 2 * (me_dp % 2)
    column = sizes["dp"] // 2

    def relay(i, peer, slot):
        return pltpu.make_async_remote_copy(
            src_ref=dsts[i].at[slot],
            dst_ref=dsts[i].at[slot],
            send_sem=send.at[i, sizes["dp"] + peer],
            recv_sem=recv.at[i, slot],
            device_id=(peer, me_ex),
            device_id_type=pl.DeviceIdType.MESH,
        )

    gathers = [i for i, (kind, _) in enumerate(plan) if kind == "gather"]
    for i in gathers:
        remote(i, partner, me_dp).start()

        @pl.loop(1, column)
        def _(k):
            remote(i, lax.rem(me_dp + 2 * k, sizes["dp"]), me_dp).start()

    for i, (kind, axis) in enumerate(plan):
        if kind == "gather":
            continue
        me, n = mine[axis], sizes[axis]

        @pl.loop(1, n)
        def _(j):
            peer = lax.rem(me + turn(j, n), n)
            remote(i, peer, me).start()

    for i in gathers:
        remote(i, partner, partner).wait_recv()

        @pl.loop(1, column)
        def _(k):
            relay(i, lax.rem(me_dp + 2 * k, sizes["dp"]), partner).start()

    for i, (kind, axis) in enumerate(plan):
        me, n = mine[axis], sizes[axis]
        if kind == "gather":
            remote(i, partner, me).wait_send()

            @pl.loop(1, column)
            def _(k):
                peer = lax.rem(me_dp + 2 * k, sizes["dp"])
                remote(i, peer, me).wait_send()
                relay(i, peer, partner).wait_send()
                remote(i, peer, peer).wait_recv()
                twin = peer + 1 - 2 * (peer % 2)
                remote(i, twin, twin).wait_recv()

            continue

        @pl.loop(1, n)
        def _(j):
            peer = lax.rem(me + turn(j, n), n)
            remote(i, peer, me).wait_send()
            remote(i, peer, peer).wait_recv()

    for copy in local:
        copy.wait()


def exchange(plan, sizes, srcs, dst_shapes, tag):
    count = len(plan)
    most = max(max(sizes.values()), 2 * sizes["dp"])
    return pl.pallas_call(
        functools.partial(xfer_kernel, plan, sizes),
        out_shape=[jax.ShapeDtypeStruct(s, a.dtype) for s, a in zip(dst_shapes, srcs)],
        in_specs=[pl.BlockSpec(memory_space=pl.ANY)] * count,
        out_specs=[pl.BlockSpec(memory_space=pl.ANY)] * count,
        scratch_shapes=[
            pltpu.SemaphoreType.DMA((count, most)),
            pltpu.SemaphoreType.DMA((count, most)),
            pltpu.SemaphoreType.DMA((count,)),
        ],
        compiler_params=pltpu.CompilerParams(collective_id=tag, has_side_effects=True),
    )(*srcs)


def per_device(tokens, routes, gates, grad_out, w_gate, w_up, w_down):
    experts = lax.axis_size("expert")
    groups = lax.axis_size("dp")
    sizes = {"dp": groups, "expert": experts}
    count = tokens.shape[0]
    width = tokens.shape[1]
    top = routes.shape[1]
    cap = 3 * count * top // (2 * experts)
    slots = experts * cap
    routed = count * top
    flat = routes.T.reshape(routed)
    route_ids = jnp.arange(routed, dtype=jnp.int32)
    same = (flat[:, None] == flat[None, :]) & (route_ids[None, :] < route_ids[:, None])
    rank = jnp.sum(same.astype(jnp.int32), axis=1)
    position = flat * cap + rank
    hit = position[None, :] == jnp.arange(slots, dtype=jnp.int32)[:, None]
    lanes = width // 128
    pick = jnp.any(hit.reshape(slots, top, count), axis=1).astype(jnp.bfloat16)
    select = (((1,), (0,)), ((), ()))
    x_send = lax.dot_general(
        pick, tokens.reshape(count, lanes, 128), select, preferred_element_type=jnp.float32
    ).astype(jnp.bfloat16)
    g_rows = lax.dot_general(
        pick, grad_out.reshape(count, lanes, 128), select, preferred_element_type=jnp.float32
    )
    slot_gate = jnp.sum(jnp.where(hit, gates.T.reshape(1, routed), 0.0), axis=1)
    s_send = (slot_gate[:, None, None] * g_rows).astype(jnp.bfloat16)
    dense = (experts, cap * lanes, 128)
    share = w_gate.shape[1]
    hid = w_gate.shape[2]
    x_in, s_in, gate_all, up_all, down_all = exchange(
        (("a2a", "expert"), ("a2a", "expert"), ("gather", "dp"), ("gather", "dp"), ("gather", "dp")),
        sizes,
        (x_send.reshape(dense), s_send.reshape(dense), w_gate[0], w_up[0], w_down[0].T),
        (dense, dense, (groups, share, hid), (groups, share, hid), (groups, share, hid)),
        0,
    )
    x3 = x_in.reshape(slots, lanes, 128)
    s3 = s_in.reshape(slots, lanes, 128)
    gate3 = gate_all.reshape(lanes, 128, hid)
    up3 = up_all.reshape(lanes, 128, hid)
    down3 = down_all.reshape(lanes, 128, hid)
    over_d = (((1, 2), (0, 1)), ((), ()))
    pre_gate = lax.dot_general(x3, gate3, over_d, preferred_element_type=jnp.float32)
    pre_up = lax.dot_general(x3, up3, over_d, preferred_element_type=jnp.float32)
    act, slope = silu_parts(pre_gate)
    hidden_f = act * pre_up
    back = lax.dot_general(s3, down3, over_d, preferred_element_type=jnp.float32)
    score = jnp.sum(back * hidden_f, axis=1).astype(jnp.bfloat16)
    d_gate = (back * pre_up * slope).astype(jnp.bfloat16)
    d_up = (back * act).astype(jnp.bfloat16)
    over_h = (((1,), (2,)), ((), ()))
    route_grad = (
        lax.dot_general(d_gate, gate3, over_h, preferred_element_type=jnp.float32)
        + lax.dot_general(d_up, up3, over_h, preferred_element_type=jnp.float32)
    ).astype(jnp.bfloat16)
    hidden = hidden_f.astype(jnp.bfloat16)
    partial = lax.dot_general(
        s3, hidden, (((0,), (0,)), ((), ())), preferred_element_type=jnp.float32
    ).astype(jnp.bfloat16)
    score_box = jnp.zeros((experts, 8, 128), jnp.bfloat16).at[:, 0, :cap].set(
        score.reshape(experts, cap)
    )
    rg_back, score_back, parts_in = exchange(
        (("a2a", "expert"), ("a2a", "expert"), ("a2a", "dp")),
        sizes,
        (route_grad.reshape(dense), score_box, partial.reshape(groups, share, hid)),
        (dense, (experts, 8, 128), (groups, share, hid)),
        1,
    )
    grad_down = jnp.sum(parts_in.astype(jnp.float32), axis=0).T[None]
    summed = lax.dot_general(
        pick, rg_back.reshape(slots, lanes, 128), (((0,), (0,)), ((), ())),
        preferred_element_type=jnp.float32,
    )
    grad_tokens = summed.astype(jnp.bfloat16).reshape(count, width)
    back_scores = score_back[:, 0, :cap].reshape(slots, 1).astype(jnp.float32)
    route_score = jnp.sum(jnp.where(hit, back_scores, 0.0), axis=0)
    grad_gates = route_score.reshape(top, count).T / gates
    return (grad_tokens, grad_gates, grad_down)


def solution(mesh):
    placed = (
        P(("dp", "expert"), None),
        P(("dp", "expert"), None),
        P(("dp", "expert"), None),
        P(("dp", "expert"), None),
        P("expert", "dp", None),
        P("expert", "dp", None),
        P("expert", None, "dp"),
    )
    return jax.shard_map(
        per_device,
        mesh=mesh,
        in_specs=placed,
        out_specs=(P(("dp", "expert"), None), P(("dp", "expert"), None), P("expert", None, "dp")),
        check_vma=False,
    )
```
